512 devices in a mesh: rows: 64 (over y, x, z_hi), cols: 8 (over z_lo, core).
Axes of the slice: x: 4, y: 8, z: 8 (z_hi: 2, z_lo: 4; z = z_hi * 4 + z_lo), core: 2. Of those that a mesh axis runs over, the one named last changes fastest.
Arguments:
- cross_kernel: float32 [65536, 1024], P('rows', 'cols'), may hold values from -6 to 6
- factor_panels: float32 [2, 512, 65536], P(None, 'cols', 'rows'), may hold values from -0.25 to 0.25
- block_inverses: float32 [2, 512, 512], P(None, 'cols'), may hold values from -0.5 to 1.5, as said below
Outputs:
- solved: float32 [65536, 1024], P('rows', 'cols')
The draws below stay inside these ranges and needn't reach their ends.
Inputs may be any that keep to these rules, and one draw needn't show every extreme that they name: `block_inverses`: each block is lower triangular, with diagonal entries from 0.5 to 1.5.
All inputs are finite; a program needn't handle non-finite values.
Results may differ from the reference program's by a relative error of at most 0.000084.
Values sent between devices are 32-bit elements; how exact they have to be, the bound alone decides.
A program may use at most 64 MiB of HBM per device.

```python
import math
import jax
import jax.numpy as jnp
from jax import lax

PANEL = 512
ROWS = 65536
CANDS = 1024


def draw_block_inverses(key, part):
    key_lower = jax.random.fold_in(key, 11)
    key_diag = jax.random.fold_in(key, 12)
    spread = 0.6 / math.sqrt(PANEL)
    lower = jax.random.normal(key_lower, (2, PANEL, PANEL), jnp.float32) * spread
    lower = jnp.clip(lower, -0.45, 0.45)
    diag = jax.random.uniform(key_diag, (2, PANEL, 1), jnp.float32, 0.5, 1.5)
    row_ids = lax.broadcasted_iota(jnp.int32, (2, PANEL, PANEL), 1)
    col_ids = lax.broadcasted_iota(jnp.int32, (2, PANEL, PANEL), 2)
    zeros = jnp.zeros((2, PANEL, PANEL), jnp.float32)
    return jnp.where(col_ids < row_ids, lower, zeros) + jnp.where(col_ids == row_ids, diag + zeros, zeros)


def steps_of(key, shape, pieces, least, top_value):
    def one(axis_at, parts):
        draws = jax.random.uniform(jax.random.fold_in(jax.random.fold_in(key, 6), axis_at), (parts,), jnp.float32, least / len(pieces), top_value / len(pieces))
        return jnp.repeat(jnp.exp(draws), shape[axis_at] // parts).reshape((-1,) + (1,) * (len(shape) - axis_at - 1))

    factor_of = one(*pieces[0])
    for cut in pieces[1:]:
        factor_of = factor_of * one(*cut)
    return factor_of


def normal_values(key, extent, deviation, most, shards=(), dtype=jnp.bfloat16):
    values = jax.random.normal(key, extent, jnp.float32) * deviation
    if len(shards) > 0:
        values = steps_of(key, extent, shards, -0.22, 0.18) * values
    return jnp.clip(values, min=-most, max=most).astype(dtype)


def setup_inputs(seed: int = 0) -> dict:
    key_list = jax.random.split(jax.random.key(seed), 4)
    cross_kernel = normal_values(key_list[0], (ROWS, CANDS), 1.0, 6.0, ((0, 64), (1, 8)), jnp.float32)
    factor_panels = normal_values(key_list[1], (2, PANEL, ROWS), PANEL ** -0.5, 0.25, ((1, 8), (2, 64)), jnp.float32)
    block_inverses = draw_block_inverses(jax.random.fold_in(key_list[3], 71), 0)
    return dict(cross_kernel=cross_kernel, factor_panels=factor_panels, block_inverses=block_inverses)


def reference(cross_kernel, factor_panels, block_inverses):
    highest = lax.Precision.HIGHEST
    width = PANEL
    first = jnp.dot(block_inverses[0], cross_kernel[:width], precision=highest, preferred_element_type=jnp.float32)
    update = lax.dot_general(factor_panels[0][:, width:], first, (((0,), (0,)), ((), ())), precision=highest, preferred_element_type=jnp.float32)
    rest = cross_kernel[width:] - update
    second = jnp.dot(block_inverses[1], rest[:width], precision=highest, preferred_element_type=jnp.float32)
    update = lax.dot_general(factor_panels[1][:, 2 * width:], second, (((0,), (0,)), ((), ())), precision=highest, preferred_element_type=jnp.float32)
    remain = rest[width:] - update
    return jnp.concatenate([first, second, remain], axis=0)
```

```python
import functools

import jax
import jax.numpy as jnp
from jax import lax
from jax.experimental import pallas as pl
from jax.experimental.pallas import tpu as pltpu
from jax.sharding import PartitionSpec as P

MESH = pl.DeviceIdType.MESH
HIGHEST = lax.Precision.HIGHEST
PLANE = 32
CHUNK = 16
HELPERS = ((1, 3, 4), (28, 5, 7))


def kernel(b_hbm, f_hbm, inv_hbm, o_ref, bv, fall, invf, fb, xb, loc, ag_s, ag_r, in_s, in_r, fb_s, fb_r, sc_s, sc_r, ex_s, ex_r):
    r, c = lax.axis_index("rows"), lax.axis_index("cols")
    m, zh = r // 2, r % 2
    zl, core = c // 2, c % 2
    sib = zl * 2 + 1 - core
    root = r == 0

    def remote(src, dst, s, rs, row, col):
        return pltpu.make_async_remote_copy(
            src_ref=src, dst_ref=dst, send_sem=s, recv_sem=rs,
            device_id={"rows": row, "cols": col}, device_id_type=MESH)

    def away(d):
        return ((zl + d) % 4) * 2 + core

    def rows_of(col):
        return pl.ds(pl.multiple_of(col * 64, 64), 64)

    mine = rows_of(c)
    get_b = pltpu.make_async_copy(b_hbm, bv, loc.at[0])
    get_f = pltpu.make_async_copy(f_hbm, fall.at[:, mine], loc.at[1])
    get_fb = pltpu.make_async_copy(f_hbm.at[0, :, pl.ds(512, 512)], fb.at[mine], loc.at[1])
    get_inv = pltpu.make_async_copy(inv_hbm, invf.at[:, mine], loc.at[2])
    get_b.start()

    @pl.when(root)
    def _():
        get_fb.start()
        get_inv.start()

    @pl.when(jnp.logical_not(root))
    def _():
        get_f.start()

    barrier = pltpu.get_barrier_semaphore()

    def tell(row, col):
        pl.semaphore_signal(barrier, inc=1, device_id={"rows": row, "cols": col}, device_id_type=MESH)

    tell(r, sib)
    for d in (1, 2, 3):
        tell(r, away(d))

    def tell_plane(j, _):
        tell(((m + j) % PLANE) * 2 + zh, c)
        return 0

    lax.fori_loop(1, PLANE, tell_plane, 0)

    @pl.when(zh == 1)
    def _():
        tell(0, c)

    @pl.when(root)
    def _():
        for p in range(2):
            for d in (1, 2, 3):
                tell(HELPERS[p][d - 1] * 2, ((zl + 4 - d) % 4) * 2 + core)
        pl.semaphore_wait(barrier, 4 + 31 + 32)

    helping = functools.reduce(jnp.logical_or, [r == h * 2 for line in HELPERS for h in line])

    @pl.when(helping)
    def _():
        pl.semaphore_wait(barrier, 4 + 31 + 1)

    @pl.when(jnp.logical_not(jnp.logical_or(root, helping)))
    def _():
        pl.semaphore_wait(barrier, 4 + 31)

    for p in range(2):
        for d in (1, 2, 3):
            @pl.when(r == HELPERS[p][d - 1] * 2)
            def _():
                remote(inv_hbm.at[p], invf.at[p, mine], in_s.at[p, d], in_r.at[p, d], 0, away(d)).start()

    def chunk(x, i):
        return xb.at[x, pl.ds(pl.multiple_of(i * CHUNK, CHUNK), CHUNK)]

    def scatter(x):
        def to_one(i, _):
            remote(chunk(x, i), chunk(x, i), sc_s.at[x, 1], sc_r.at[x], i * 2 + 1, c).start()

            @pl.when(i > 0)
            def _():
                remote(chunk(x, i), chunk(x, i), sc_s.at[x, 0], sc_r.at[x], i * 2, c).start()
            return 0

        lax.fori_loop(0, PLANE, to_one, 0)

    def exchange(x):
        def to_one(j, _):
            peer = ((m + j) % PLANE) * 2 + zh

            @pl.when(peer > 0)
            def _():
                remote(chunk(x, m), chunk(x, m), ex_s.at[x], ex_r.at[x], peer, c).start()
            return 0

        lax.fori_loop(1, PLANE, to_one, 0)

    def first_rows(x, n):
        return xb.at[x, pl.ds(0, n * CHUNK)]

    def blocks_across(value):
        return jnp.concatenate([value[i * 128:(i + 1) * 128].T for i in range(4)], axis=0)

    @pl.when(root)
    def _():
        get_inv.wait()
        get_fb.wait()
        own_inv = [remote(invf.at[p, mine], invf.at[p, mine], in_s.at[p, 0], in_r.at[p, 0], 0, sib) for p in range(2)]
        own_fb = [remote(fb.at[mine], fb.at[mine], fb_s.at[d], fb_r.at[d], 0, sib if d == 0 else away(d)) for d in range(4)]
        for copy in own_inv + own_fb:
            copy.start()
        relays = []

        def relay(ref_of, s, rs, arrive_s, arrive_r):
            for d in (1, 2, 3):
                got = ref_of(rows_of(away(4 - d)))
                remote(got, got, arrive_s.at[d], arrive_r.at[d], 0, sib).wait_recv()
                on = remote(got, got, s.at[d + 3], rs.at[d + 3], 0, sib)
                on.start()
                relays.append(on)

        for p in range(2):
            relay(lambda rows: invf.at[p, rows], in_s.at[p], in_r.at[p], in_s.at[p], in_r.at[p])
        own_inv[0].wait_recv()
        for copy in relays[:3]:
            copy.wait_recv()
        get_b.wait()
        first = jnp.dot(invf[0], bv[0:512], precision=HIGHEST, preferred_element_type=jnp.float32)
        o_ref[0:512] = first
        xb[0] = blocks_across(first)
        scatter(0)
        exchange(0)
        relay(lambda rows: fb.at[rows], fb_s, fb_r, fb_s, fb_r)
        own_fb[0].wait_recv()
        for copy in relays[6:]:
            copy.wait_recv()
        rest = bv[512:1024] - lax.dot_general(
            fb[...], o_ref[0:512], (((0,), (0,)), ((), ())), precision=HIGHEST, preferred_element_type=jnp.float32)
        own_inv[1].wait_recv()
        for copy in relays[3:6]:
            copy.wait_recv()
        second = jnp.dot(invf[1], rest, precision=HIGHEST, preferred_element_type=jnp.float32)
        o_ref[512:1024] = second
        xb[1] = blocks_across(second)
        scatter(1)
        exchange(1)
        for copy in own_inv + own_fb + relays:
            copy.wait_send()
        for x in range(2):
            remote(first_rows(x, 31), first_rows(x, 31), sc_s.at[x, 0], sc_r.at[x], 1, c).wait_send()
            remote(first_rows(x, 32), first_rows(x, 32), sc_s.at[x, 1], sc_r.at[x], 1, c).wait_send()
            remote(first_rows(x, 31), first_rows(x, 31), ex_s.at[x], ex_r.at[x], 1, c).wait_send()

    @pl.when(jnp.logical_not(root))
    def _():
        get_f.wait()
        own = [remote(fall.at[:, mine], fall.at[:, mine], ag_s.at[d], ag_r.at[d], r, sib if d == 0 else away(d)) for d in range(4)]
        for copy in own:
            copy.start()
        for x in range(2):
            remote(chunk(x, m), chunk(x, m), sc_s.at[x, 0], sc_r.at[x], 0, c).wait_recv()
            exchange(x)
        relays = []
        for d in (1, 2, 3):
            own[d].wait_recv()
            got = fall.at[:, rows_of(away(4 - d))]
            on = remote(got, got, ag_s.at[d + 3], ag_r.at[d + 3], r, sib)
            on.start()
            relays.append(on)
        own[0].wait_recv()
        for copy in relays:
            copy.wait_recv()
        get_b.wait()
        for x in range(2):
            remote(first_rows(x, 31), first_rows(x, 31), ex_s.at[x], ex_r.at[x], 0, c).wait_recv()
            left = jnp.concatenate([xb[x, i * 128:(i + 1) * 128] for i in range(4)], axis=1)
            src = bv if x == 0 else o_ref

            def update(i, _):
                cut = pl.ds(pl.multiple_of(i * 256, 256), 256)
                took = jnp.dot(left, fall[x, :, cut], precision=HIGHEST, preferred_element_type=jnp.float32)
                o_ref[cut] = src[cut] - took.T
                return 0

            lax.fori_loop(0, 4, update, 0)
        for copy in own + relays:
            copy.wait_send()
        for p in range(2):
            for d in (1, 2, 3):
                @pl.when(r == HELPERS[p][d - 1] * 2)
                def _():
                    remote(inv_hbm.at[p], invf.at[p, mine], in_s.at[p, d], in_r.at[p, d], 0, away(d)).wait_send()
        for x in range(2):
            @pl.when(zh == 0)
            def _():
                remote(first_rows(x, 30), first_rows(x, 30), ex_s.at[x], ex_r.at[x], 1, c).wait_send()

            @pl.when(zh == 1)
            def _():
                remote(first_rows(x, 31), first_rows(x, 31), ex_s.at[x], ex_r.at[x], 1, c).wait_send()


def on_device(cross_kernel, factor_panels, block_inverses):
    dma = pltpu.SemaphoreType.DMA
    any_space = pl.BlockSpec(memory_space=pl.ANY)
    return pl.pallas_call(
        kernel,
        out_shape=jax.ShapeDtypeStruct(cross_kernel.shape, jnp.float32),
        in_specs=[any_space] * 3,
        out_specs=pl.BlockSpec(memory_space=pltpu.VMEM),
        scratch_shapes=[
            pltpu.VMEM((1024, 128), jnp.float32),
            pltpu.VMEM((2, 512, 1024), jnp.float32),
            pltpu.VMEM((2, 512, 512), jnp.float32),
            pltpu.VMEM((512, 512), jnp.float32),
            pltpu.VMEM((2, 512, 128), jnp.float32),
            dma((3,)),
            dma((7,)), dma((7,)),
            dma((2, 7)), dma((2, 7)),
            dma((7,)), dma((7,)),
            dma((2, 2)), dma((2,)),
            dma((2,)), dma((2,)),
        ],
        compiler_params=pltpu.CompilerParams(
            collective_id=0, has_side_effects=True, vmem_limit_bytes=48 << 20),
    )(cross_kernel, factor_panels, block_inverses)


def solution(mesh):
    in_specs = (P("rows", "cols"), P(None, "cols", "rows"), P(None, "cols", None))
    out_specs = P("rows", "cols")
    return jax.shard_map(
        on_device, mesh=mesh, in_specs=in_specs, out_specs=out_specs, check_vma=False
    )
```

```python
import jax
import jax.numpy as jnp
from jax import lax
from jax.experimental import pallas as pl
from jax.experimental.pallas import tpu as pltpu
from jax.sharding import PartitionSpec as P

MESH = pl.DeviceIdType.MESH
HIGHEST = lax.Precision.HIGHEST
PLANE = 32
CHUNK = 16


def kernel(b_hbm, f_hbm, inv_hbm, o_ref, bv, fall, invf, fb, xb, loc, ag_s, ag_r, sb_s, sb_r, in_s, in_r, fb_s, fb_r, sc_s, sc_r, ex_s, ex_r, ready):
    r, c = lax.axis_index("rows"), lax.axis_index("cols")
    m, zh = r // 2, r % 2
    zl, core = c // 2, c % 2
    sib = zl * 2 + 1 - core
    root = r == 0
    other = jnp.logical_not(root)

    def remote(src, dst, s, rs, row, col):
        return pltpu.make_async_remote_copy(
            src_ref=src, dst_ref=dst, send_sem=s, recv_sem=rs,
            device_id={"rows": row, "cols": col}, device_id_type=MESH)

    def away(d):
        return ((zl + d) % 4) * 2 + core

    def rows_of(col):
        return pl.ds(pl.multiple_of(col * 64, 64), 64)

    duty = m - 1
    duty_p, duty_d = duty // 12, duty % 3 + 1
    helping = (zh == 0) & (m >= 1) & (m <= 24) & ((duty % 12) // 3 == zl)

    mine = rows_of(c)
    get_b = pltpu.make_async_copy(b_hbm, bv, loc.at[0])
    get_f = pltpu.make_async_copy(f_hbm, fall.at[:, mine], loc.at[1])
    get_fb = pltpu.make_async_copy(f_hbm.at[0, :, pl.ds(512, 512)], fb.at[mine], loc.at[1])
    get_inv = pltpu.make_async_copy(inv_hbm, invf.at[:, mine], loc.at[2])
    barrier = pltpu.get_barrier_semaphore()

    def tell(row, col):
        pl.semaphore_signal(barrier, inc=1, device_id={"rows": row, "cols": col}, device_id_type=MESH)

    tell(r, sib)
    for d in (1, 2, 3):
        tell(r, away(d))

    @pl.when(root)
    def _():
        get_inv.start()
        get_fb.start()
        for p in range(2):
            for d in (1, 2, 3):
                source = (zl + 4 - d) % 4
                tell((p * 12 + source * 3 + d) * 2, source * 2 + core)

        def tell_all(j, _):
            tell(j, c)
            return 0

        lax.fori_loop(1, 2 * PLANE, tell_all, 0)
        get_b.start()
        pl.semaphore_wait(barrier, 4)

    @pl.when(other)
    def _():
        get_f.start()
        get_b.start()

        def tell_plane(j, _):
            peer = ((m + j) % PLANE) * 2 + zh

            @pl.when(peer > 0)
            def _():
                tell(peer, c)
            return 0

        lax.fori_loop(1, PLANE, tell_plane, 0)
        pl.semaphore_wait(barrier, 4 + 30 + zh + 1 + helping.astype(jnp.int32))

    duty_copy = remote(inv_hbm.at[duty_p], invf.at[duty_p, mine], in_s.at[duty_p, duty_d], in_r.at[duty_p, duty_d], 0, away(duty_d))
    @pl.when(helping)
    def _():
        duty_copy.start()

    def chunk(x, i):
        return xb.at[x, pl.ds(pl.multiple_of(i * CHUNK, CHUNK), CHUNK)]

    def scatter(x):
        def to_one(i, _):
            remote(chunk(x, i), chunk(x, i), sc_s.at[x, 1], sc_r.at[x], i * 2 + 1, c).start()

            @pl.when(i > 0)
            def _():
                remote(chunk(x, i), chunk(x, i), sc_s.at[x, 0], sc_r.at[x], i * 2, c).start()
            return 0

        lax.fori_loop(0, PLANE, to_one, 0)

    def exchange(x):
        def to_one(j, _):
            peer = ((m + j) % PLANE) * 2 + zh

            @pl.when(peer > 0)
            def _():
                remote(chunk(x, m), chunk(x, m), ex_s.at[x], ex_r.at[x], peer, c).start()
            return 0

        lax.fori_loop(1, PLANE, to_one, 0)

    def first_rows(x, n):
        return xb.at[x, pl.ds(0, n * CHUNK)]

    def blocks_across(value):
        return jnp.concatenate([value[i * 128:(i + 1) * 128].T for i in range(4)], axis=0)

    @pl.when(root)
    def _():
        get_inv.wait()
        own_inv = [remote(invf.at[p, mine], invf.at[p, mine], in_s.at[p, 0], in_r.at[p, 0], 0, sib) for p in range(2)]
        own_fb = [remote(fb.at[mine], fb.at[mine], fb_s.at[d], fb_r.at[d], 0, sib if d == 0 else away(d)) for d in range(4)]
        own_inv[0].start()
        get_fb.wait()
        for copy in own_fb + own_inv[1:]:
            copy.start()
        relays = []

        def relay(ref_of, s, rs):
            for d in (1, 2, 3):
                got = ref_of(rows_of(away(4 - d)))
                remote(got, got, s.at[d], rs.at[d], 0, sib).wait_recv()
                on = remote(got, got, s.at[d + 3], rs.at[d + 3], 0, sib)
                on.start()
                relays.append(on)

        for p in range(2):
            relay(lambda rows: invf.at[p, rows], in_s.at[p], in_r.at[p])
        own_inv[0].wait_recv()
        for copy in relays[:3]:
            copy.wait_recv()
        get_b.wait()
        first = jnp.dot(invf[0], bv[0:512], precision=HIGHEST, preferred_element_type=jnp.float32)
        o_ref[0:512] = first
        xb[0] = blocks_across(first)
        pl.semaphore_wait(ready, 63)
        scatter(0)
        exchange(0)
        relay(lambda rows: fb.at[rows], fb_s, fb_r)
        own_fb[0].wait_recv()
        for copy in relays[6:]:
            copy.wait_recv()
        rest = bv[512:1024] - lax.dot_general(
            fb[...], o_ref[0:512], (((0,), (0,)), ((), ())), precision=HIGHEST, preferred_element_type=jnp.float32)
        own_inv[1].wait_recv()
        for copy in relays[3:6]:
            copy.wait_recv()
        second = jnp.dot(invf[1], rest, precision=HIGHEST, preferred_element_type=jnp.float32)
        o_ref[512:1024] = second
        xb[1] = blocks_across(second)
        scatter(1)
        exchange(1)
        for copy in own_inv + own_fb + relays:
            copy.wait_send()
        for x in range(2):
            remote(first_rows(x, 31), first_rows(x, 31), sc_s.at[x, 0], sc_r.at[x], 1, c).wait_send()
            remote(first_rows(x, 32), first_rows(x, 32), sc_s.at[x, 1], sc_r.at[x], 1, c).wait_send()
            remote(first_rows(x, 31), first_rows(x, 31), ex_s.at[x], ex_r.at[x], 1, c).wait_send()

    def has_source(way, step):
        return zl >= step + 1 if way == 0 else zl <= 2 - step

    def has_target(way):
        return zl <= 2 if way == 0 else zl >= 1

    def shard_at(way, step, p):
        return fall.at[p, rows_of(away(3 - step if way == 0 else 1 + step))]

    def along(way, step, p):
        piece = fall.at[p, mine] if step == 0 else shard_at(way, step - 1, p)
        return remote(piece, piece, ag_s.at[way, step, p], ag_r.at[way, step, p], r, away(1 if way == 0 else 3))

    def arrived(way, step, p):
        piece = shard_at(way, step, p)
        return remote(piece, piece, ag_s.at[way, step, p], ag_r.at[way, step, p], r, sib)

    def across(way, step, p):
        piece = shard_at(way, step, p)
        return remote(piece, piece, sb_s.at[1 + way * 3 + step, p], sb_r.at[1 + way * 3 + step, p], r, sib)

    def own_across(p):
        return remote(fall.at[p, mine], fall.at[p, mine], sb_s.at[0, p], sb_r.at[0, p], r, sib)

    def take(step, p):
        for way in range(2):
            @pl.when(has_source(way, step))
            def _():
                arrived(way, step, p).wait_recv()
                if step < 2:
                    @pl.when(has_target(way))
                    def _():
                        along(way, step + 1, p).start()
                across(way, step, p).start()

    @pl.when(other)
    def _():
        pl.semaphore_signal(ready, inc=1, device_id={"rows": 0, "cols": c}, device_id_type=MESH)
        get_f.wait()
        for p in range(2):
            for way in range(2):
                @pl.when(has_target(way))
                def _():
                    along(way, 0, p).start()
        for p in range(2):
            own_across(p).start()
        take(0, 0)
        take(0, 1)

        def solved(x):
            remote(chunk(x, m), chunk(x, m), sc_s.at[x, 0], sc_r.at[x], 0, c).wait_recv()
            exchange(x)

        solved(0)
        take(1, 0)
        take(1, 1)
        solved(1)
        get_b.wait()
        for x in range(2):
            take(2, x)
            own_across(x).wait_recv()
            for step in range(3):
                for way in range(2):
                    @pl.when(has_source(way, step))
                    def _():
                        across(way, step, x).wait_recv()
            remote(first_rows(x, 31), first_rows(x, 31), ex_s.at[x], ex_r.at[x], 0, c).wait_recv()
            left = jnp.concatenate([xb[x, i * 128:(i + 1) * 128] for i in range(4)], axis=1)
            src = bv if x == 0 else o_ref

            def update(i, _):
                cut = pl.ds(pl.multiple_of(i * 256, 256), 256)
                took = jnp.dot(left, fall[x, :, cut], precision=HIGHEST, preferred_element_type=jnp.float32)
                o_ref[cut] = src[cut] - took.T
                return 0

            lax.fori_loop(0, 4, update, 0)
        for p in range(2):
            own_across(p).wait_send()
            for way in range(2):
                for step in range(3):
                    @pl.when(has_source(way, step))
                    def _():
                        across(way, step, p).wait_send()
                    sent = has_target(way) if step == 0 else has_target(way) & has_source(way, step - 1)

                    @pl.when(sent)
                    def _():
                        along(way, step, p).wait_send()
        @pl.when(helping)
        def _():
            duty_copy.wait_send()
        for x in range(2):
            @pl.when(zh == 0)
            def _():
                remote(first_rows(x, 30), first_rows(x, 30), ex_s.at[x], ex_r.at[x], 1, c).wait_send()

            @pl.when(zh == 1)
            def _():
                remote(first_rows(x, 31), first_rows(x, 31), ex_s.at[x], ex_r.at[x], 1, c).wait_send()


def on_device(cross_kernel, factor_panels, block_inverses):
    dma = pltpu.SemaphoreType.DMA
    any_space = pl.BlockSpec(memory_space=pl.ANY)
    return pl.pallas_call(
        kernel,
        out_shape=jax.ShapeDtypeStruct(cross_kernel.shape, jnp.float32),
        in_specs=[any_space] * 3,
        out_specs=pl.BlockSpec(memory_space=pltpu.VMEM),
        scratch_shapes=[
            pltpu.VMEM((1024, 128), jnp.float32),
            pltpu.VMEM((2, 512, 1024), jnp.float32),
            pltpu.VMEM((2, 512, 512), jnp.float32),
            pltpu.VMEM((512, 512), jnp.float32),
            pltpu.VMEM((2, 512, 128), jnp.float32),
            dma((3,)),
            dma((2, 3, 2)), dma((2, 3, 2)),
            dma((7, 2)), dma((7, 2)),
            dma((2, 7)), dma((2, 7)),
            dma((7,)), dma((7,)),
            dma((2, 2)), dma((2,)),
            dma((2,)), dma((2,)),
            pltpu.SemaphoreType.REGULAR,
        ],
        compiler_params=pltpu.CompilerParams(
            collective_id=0, has_side_effects=True, vmem_limit_bytes=60 << 20),
    )(cross_kernel, factor_panels, block_inverses)


def solution(mesh):
    in_specs = (P("rows", "cols"), P(None, "cols", "rows"), P(None, "cols", None))
    out_specs = P("rows", "cols")
    return jax.shard_map(
        on_device, mesh=mesh, in_specs=in_specs, out_specs=out_specs, check_vma=False
    )
```

```python
import jax
import jax.numpy as jnp
from jax import lax
from jax.experimental import pallas as pl
from jax.experimental.pallas import tpu as pltpu
from jax.sharding import PartitionSpec as P

MESH = pl.DeviceIdType.MESH
PLANE = 32
CHUNK = 16
FLOWS = tuple(
    (p, source, target, 2 * lines[p] + (abs(source - target) == 3))
    for source, target, lines in (
        (1, 0, (2, 2)), (2, 0, (3, 1)), (3, 0, (1, 3)),
        (0, 1, (1, 2)), (2, 1, (2, 3)), (3, 1, (3, 1)),
        (0, 2, (3, 2)), (1, 2, (1, 3)), (3, 2, (2, 1)),
        (0, 3, (1, 3)), (1, 3, (2, 2)), (2, 3, (3, 1)),
    )
    for p in range(2)
)


def halves(value):
    high = value.astype(jnp.bfloat16)
    return high, (value - high.astype(jnp.float32)).astype(jnp.bfloat16)


def product(left, right):
    (a, b), (c, d) = halves(left), halves(right)
    dot = lambda x, y: jnp.dot(x, y, preferred_element_type=jnp.float32)
    return dot(a, c) + (dot(a, d) + dot(b, c))


def kernel(b_hbm, f_hbm, inv_hbm, o_ref, bv, fall, invf, fb, xb, total, loc, ag_s, ag_r, sb_s, sb_r, in_s, in_r, on_s, on_r, fb_s, fb_r, sc_s, sc_r, ex_s, ex_r, ready):
    r, c = lax.axis_index("rows"), lax.axis_index("cols")
    m, zh = r // 2, r % 2
    zl, core = c // 2, c % 2
    sib = zl * 2 + 1 - core
    root = r == 0
    other = jnp.logical_not(root)

    def remote(src, dst, s, rs, row, col):
        return pltpu.make_async_remote_copy(
            src_ref=src, dst_ref=dst, send_sem=s, recv_sem=rs,
            device_id={"rows": row, "cols": col}, device_id_type=MESH)

    def away(d):
        return ((zl + d) % 4) * 2 + core

    def rows_of(col):
        return pl.ds(pl.multiple_of(col * 64, 64), 64)

    mine = rows_of(c)
    get_b = pltpu.make_async_copy(b_hbm, bv, loc.at[0])
    get_f = pltpu.make_async_copy(f_hbm, fall.at[:, mine], loc.at[1])
    get_fb = pltpu.make_async_copy(f_hbm.at[0, :, pl.ds(512, 512)], fb.at[mine], loc.at[1])
    get_inv = pltpu.make_async_copy(inv_hbm, invf.at[:, mine], loc.at[2])
    barrier = pltpu.get_barrier_semaphore()

    def tell(row, col):
        pl.semaphore_signal(barrier, inc=1, device_id={"rows": row, "cols": col}, device_id_type=MESH)

    for d in (1, 2, 3):
        tell(r, away(d))
    tell(r, sib)

    @pl.when(root)
    def _():
        get_fb.start()
        get_inv.start()
        for p, source, target, row in FLOWS:
            @pl.when(zl == target)
            def _():
                tell(row, source * 2 + core)

        def tell_all(j, _):
            tell(2 * PLANE - j, c)
            return 0

        lax.fori_loop(1, 2 * PLANE, tell_all, 0)
        get_b.start()
        pl.semaphore_wait(barrier, 4)

    @pl.when(other)
    def _():
        get_f.start()
        get_b.start()
        duties = sum(((r == row) & (zl == source)).astype(jnp.int32) for p, source, target, row in FLOWS)
        pl.semaphore_wait(barrier, 4 + 1 + duties)
        pl.semaphore_signal(ready, inc=1, device_id={"rows": 0, "cols": c}, device_id_type=MESH)

    def inverse_rows(p, source, core_of):
        return (p, pl.ds(pl.multiple_of(source * 128 + core_of * 64, 64), 64), pl.ds(0, (source + 1) * 128))

    def duty(p, source, target):
        return remote(
            inv_hbm.at[p, :, pl.ds(0, (source + 1) * 128)], invf.at[inverse_rows(p, source, core)],
            in_s.at[p, target], in_r.at[p, source], 0, target * 2 + core)

    for p, source, target, row in FLOWS:
        @pl.when((r == row) & (zl == source))
        def _():
            duty(p, source, target).start()

    def chunk(x, i):
        return xb.at[x, pl.ds(pl.multiple_of(i * CHUNK, CHUNK), CHUNK)]

    def scatter(x):
        def to_one(i, _):
            remote(chunk(x, i), chunk(x, i), sc_s.at[x, 1], sc_r.at[x], i * 2 + 1, c).start()

            @pl.when(i > 0)
            def _():
                remote(chunk(x, i), chunk(x, i), sc_s.at[x, 0], sc_r.at[x], i * 2, c).start()
            return 0

        lax.fori_loop(0, PLANE, to_one, 0)

    def exchange(x):
        def to_one(j, _):
            peer = ((m + j) % PLANE) * 2 + zh

            @pl.when(peer > 0)
            def _():
                remote(chunk(x, m), chunk(x, m), ex_s.at[x], ex_r.at[x], peer, c).start()
            return 0

        lax.fori_loop(1, PLANE, to_one, 0)

    def first_rows(x, n):
        return xb.at[x, pl.ds(0, n * CHUNK)]

    @pl.when(root)
    def _():
        get_fb.wait()
        own_fb = [remote(fb.at[mine], fb.at[mine], fb_s.at[d], fb_r.at[d], 0, sib if d == 0 else away(d)) for d in range(4)]
        for copy in own_fb[1:] + own_fb[:1]:
            copy.start()
        get_inv.wait()

        def inverse_on(p, source, core_of):
            piece = invf.at[inverse_rows(p, source, core_of)]
            return remote(piece, piece, on_s.at[p, source], on_r.at[p, source], 0, sib)

        def inverse_arrived(p, source):
            @pl.when(zl != source)
            def _():
                piece = invf.at[inverse_rows(p, source, core)]
                remote(piece, piece, in_s.at[p, 0], in_r.at[p, source], 0, sib).wait_recv()
            inverse_on(p, source, core).start()

        def inverse_times(p, source, right):
            inverse_on(p, source, 1 - core).wait_recv()
            return product(invf[p, source * 128:(source + 1) * 128, 0:(source + 1) * 128], right)

        for i in range(4):
            inverse_arrived(0, i)
        get_b.wait()
        for i in range(4):
            block = inverse_times(0, i, bv[0:(i + 1) * 128])
            o_ref[i * 128:(i + 1) * 128] = block
            xb[0, i * 128:(i + 1) * 128] = block.T
        pl.semaphore_wait(ready, 63)
        scatter(0)
        fb_on = []
        for d in (1, 2, 3):
            got = fb.at[rows_of(away(4 - d))]
            remote(got, got, fb_s.at[d], fb_r.at[d], 0, sib).wait_recv()
            on = remote(got, got, fb_s.at[d + 3], fb_r.at[d + 3], 0, sib)
            on.start()
            fb_on.append(on)
        for i in range(4):
            inverse_arrived(1, i)
        own_fb[0].wait_recv()
        for copy in fb_on:
            copy.wait_recv()
        for i in range(4):
            cut = slice(i * 128, (i + 1) * 128)
            took = product(fb[:, cut].T, o_ref[0:512])
            bv[512 + i * 128:512 + (i + 1) * 128] = bv[512 + i * 128:512 + (i + 1) * 128] - took
        for i in range(4):
            block = inverse_times(1, i, bv[512:512 + (i + 1) * 128])
            o_ref[512 + i * 128:512 + (i + 1) * 128] = block
            xb[1, i * 128:(i + 1) * 128] = block.T
        scatter(1)
        exchange(1)
        exchange(0)
        for copy in own_fb + fb_on:
            copy.wait_send()
        for p in range(2):
            for i in range(4):
                inverse_on(p, i, core).wait_send()
        for x in range(2):
            remote(first_rows(x, 31), first_rows(x, 31), sc_s.at[x, 0], sc_r.at[x], 1, c).wait_send()
            remote(first_rows(x, 32), first_rows(x, 32), sc_s.at[x, 1], sc_r.at[x], 1, c).wait_send()
            remote(first_rows(x, 31), first_rows(x, 31), ex_s.at[x], ex_r.at[x], 1, c).wait_send()

    def has_source(way, step):
        return zl >= step + 1 if way == 0 else zl <= 2 - step

    def has_target(way):
        return zl <= 2 if way == 0 else zl >= 1

    def shard_at(way, step, p):
        return fall.at[p, rows_of(away(3 - step if way == 0 else 1 + step))]

    def along(way, step, p):
        piece = fall.at[p, mine] if step == 0 else shard_at(way, step - 1, p)
        return remote(piece, piece, ag_s.at[way, step, p], ag_r.at[way, step, p], r, away(1 if way == 0 else 3))

    def arrived(way, step, p):
        piece = shard_at(way, step, p)
        return remote(piece, piece, ag_s.at[way, step, p], ag_r.at[way, step, p], r, sib)

    def across(way, step, p):
        piece = shard_at(way, step, p)
        return remote(piece, piece, sb_s.at[1 + way * 3 + step, p], sb_r.at[1 + way * 3 + step, p], r, sib)

    def own_across(p):
        return remote(fall.at[p, mine], fall.at[p, mine], sb_s.at[0, p], sb_r.at[0, p], r, sib)

    def take(step, p):
        for way in range(2):
            @pl.when(has_source(way, step))
            def _():
                arrived(way, step, p).wait_recv()
                if step < 2:
                    @pl.when(has_target(way))
                    def _():
                        along(way, step + 1, p).start()
                across(way, step, p).start()

    @pl.when(other)
    def _():
        get_f.wait()
        for p in range(2):
            for way in range(2):
                @pl.when(has_target(way))
                def _():
                    along(way, 0, p).start()
        for p in range(2):
            own_across(p).start()
        take(0, 0)
        take(0, 1)

        def solved(x):
            remote(chunk(x, m), chunk(x, m), sc_s.at[x, 0], sc_r.at[x], 0, c).wait_recv()
            exchange(x)

        solved(0)
        take(1, 0)
        take(1, 1)
        solved(1)
        get_b.wait()
        for x in range(2):
            take(2, x)
            own_across(x).wait_recv()
            for step in range(3):
                for way in range(2):
                    @pl.when(has_source(way, step))
                    def _():
                        across(way, step, x).wait_recv()
            remote(first_rows(x, 31), first_rows(x, 31), ex_s.at[x], ex_r.at[x], 0, c).wait_recv()
            left = jnp.concatenate([xb[x, i * 128:(i + 1) * 128] for i in range(4)], axis=1)

            def update(i, _):
                cut = pl.ds(pl.multiple_of(i * 256, 256), 256)
                took = product(left, fall[x, :, cut])
                if x == 0:
                    total[:, cut] = took
                else:
                    o_ref[cut] = bv[cut] - (total[:, cut] + took).T
                return 0

            lax.fori_loop(0, 4, update, 0)
        for p in range(2):
            own_across(p).wait_send()
            for way in range(2):
                for step in range(3):
                    @pl.when(has_source(way, step))
                    def _():
                        across(way, step, p).wait_send()
                    sent = has_target(way) if step == 0 else has_target(way) & has_source(way, step - 1)

                    @pl.when(sent)
                    def _():
                        along(way, step, p).wait_send()
        for p, source, target, row in FLOWS:
            @pl.when((r == row) & (zl == source))
            def _():
                duty(p, source, target).wait_send()
        for x in range(2):
            @pl.when(zh == 0)
            def _():
                remote(first_rows(x, 30), first_rows(x, 30), ex_s.at[x], ex_r.at[x], 1, c).wait_send()

            @pl.when(zh == 1)
            def _():
                remote(first_rows(x, 31), first_rows(x, 31), ex_s.at[x], ex_r.at[x], 1, c).wait_send()


def on_device(cross_kernel, factor_panels, block_inverses):
    dma = pltpu.SemaphoreType.DMA
    any_space = pl.BlockSpec(memory_space=pl.ANY)
    return pl.pallas_call(
        kernel,
        out_shape=jax.ShapeDtypeStruct(cross_kernel.shape, jnp.float32),
        in_specs=[any_space] * 3,
        out_specs=pl.BlockSpec(memory_space=pltpu.VMEM),
        scratch_shapes=[
            pltpu.VMEM((1024, 128), jnp.float32),
            pltpu.VMEM((2, 512, 1024), jnp.float32),
            pltpu.VMEM((2, 512, 512), jnp.float32),
            pltpu.VMEM((512, 512), jnp.float32),
            pltpu.VMEM((2, 512, 128), jnp.float32),
            pltpu.VMEM((128, 1024), jnp.float32),
            dma((3,)),
            dma((2, 3, 2)), dma((2, 3, 2)),
            dma((7, 2)), dma((7, 2)),
            dma((2, 4)), dma((2, 4)),
            dma((2, 4)), dma((2, 4)),
            dma((7,)), dma((7,)),
            dma((2, 2)), dma((2,)),
            dma((2,)), dma((2,)),
            pltpu.SemaphoreType.REGULAR,
        ],
        compiler_params=pltpu.CompilerParams(
            collective_id=0, has_side_effects=True, vmem_limit_bytes=48 << 20),
    )(*[pltpu.with_memory_space_constraint(x, pltpu.HBM) for x in (cross_kernel, factor_panels, block_inverses)])


def solution(mesh):
    in_specs = (P("rows", "cols"), P(None, "cols", "rows"), P(None, "cols", None))
    out_specs = P("rows", "cols")
    return jax.shard_map(
        on_device, mesh=mesh, in_specs=in_specs, out_specs=out_specs, check_vma=False
    )
```

```python
import jax
import jax.numpy as jnp
from jax import lax
from jax.experimental import pallas as pl
from jax.experimental.pallas import tpu as pltpu
from jax.sharding import PartitionSpec as P

MESH = pl.DeviceIdType.MESH
PLANE = 32
CHUNK = 16
STRIDE = 13
FLOWS = tuple(
    (p, source, target, lines[p])
    for source, target, lines in (
        (1, 0, (0, 4)), (2, 0, (0, 3)), (3, 0, (3, 7)),
        (0, 1, (4, 2)), (2, 1, (2, 6)), (3, 1, (5, 7)),
        (0, 2, (7, 5)), (1, 2, (6, 4)), (3, 2, (2, 4)),
        (0, 3, (3, 5)), (1, 3, (0, 7)), (2, 3, (0, 2)),
    )
    for p in range(2)
)


def halves(value):
    high = value.astype(jnp.bfloat16)
    return high, (value - high.astype(jnp.float32)).astype(jnp.bfloat16)


def product(left, right):
    (a, b), (c, d) = halves(left), halves(right)
    dot = lambda x, y: jnp.dot(x, y, preferred_element_type=jnp.float32)
    return dot(a, c) + (dot(a, d) + dot(b, c))


def kernel(b_hbm, f_hbm, inv_hbm, o_ref, bv, fall, invf, fb, xb, total, loc, ag_s, ag_r, sb_s, sb_r, in_s, in_r, on_s, on_r, fb_s, fb_r, sc_s, sc_r, ex_s, ex_r, ready, above):
    r, c = lax.axis_index("rows"), lax.axis_index("cols")
    m, zh = r // 2, r % 2
    zl, core = c // 2, c % 2
    sib = zl * 2 + 1 - core
    root = r == 0
    other = jnp.logical_not(root)

    def remote(src, dst, s, rs, row, col):
        return pltpu.make_async_remote_copy(
            src_ref=src, dst_ref=dst, send_sem=s, recv_sem=rs,
            device_id={"rows": row, "cols": col}, device_id_type=MESH)

    def away(d):
        return ((zl + d) % 4) * 2 + core

    def rows_of(col):
        return pl.ds(pl.multiple_of(col * 64, 64), 64)

    mine = rows_of(c)
    get_b = pltpu.make_async_copy(b_hbm, bv, loc.at[0])
    get_f = pltpu.make_async_copy(f_hbm, fall.at[:, mine], loc.at[1])
    get_fb = pltpu.make_async_copy(f_hbm.at[0, :, pl.ds(512, 512)], fb.at[mine], loc.at[1])
    get_inv = pltpu.make_async_copy(inv_hbm, invf.at[:, mine], loc.at[2])
    barrier = pltpu.get_barrier_semaphore()

    def tell(row, col):
        pl.semaphore_signal(barrier, inc=1, device_id={"rows": row, "cols": col}, device_id_type=MESH)

    tell(r, sib)

    def open_down(reach):
        for d in range(1, reach + 1):
            @pl.when(zl >= d)
            def _():
                pl.semaphore_signal(above, inc=1, device_id={"rows": r, "cols": c - 2 * d}, device_id_type=MESH)

    @pl.when(root)
    def _():
        for d in range(1, 4):
            @pl.when(zl + d <= 3)
            def _():
                tell(r, c + 2 * d)
        get_fb.start()
        get_inv.start()
        for p, source, target, row in FLOWS:
            if row > 0:
                @pl.when(zl == target)
                def _():
                    tell(row, source * 2 + core)

        def tell_all(j, _):
            tell(2 * PLANE - j, c)
            return 0

        lax.fori_loop(1, 2 * PLANE, tell_all, 0)
        get_b.start()
        pl.semaphore_wait(barrier, zl + 1)
        open_down(3)

    @pl.when(other)
    def _():
        @pl.when(zl < 3)
        def _():
            tell(r, c + 2)
        get_f.start()
        get_b.start()
        duties = sum(((r == row) & (zl == source)).astype(jnp.int32) for p, source, target, row in FLOWS if row > 0)
        pl.semaphore_wait(barrier, jnp.minimum(zl, 1) + 1 + 1 + duties)
        open_down(1)
        pl.semaphore_signal(ready, inc=1, device_id={"rows": 0, "cols": c}, device_id_type=MESH)

    def inverse_rows(p, source, core_of):
        return (p, pl.ds(pl.multiple_of(source * 128 + core_of * 64, 64), 64), pl.ds(0, (source + 1) * 128))

    def duty(p, source, target):
        return remote(
            inv_hbm.at[p, :, pl.ds(0, (source + 1) * 128)], invf.at[inverse_rows(p, source, core)],
            in_s.at[p, target], in_r.at[p, source], 0, target * 2 + core)

    for p, source, target, row in FLOWS:
        if row > 0:
            @pl.when((r == row) & (zl == source))
            def _():
                duty(p, source, target).start()

    def chunk(x, i):
        return xb.at[x, pl.ds(pl.multiple_of(i * CHUNK, CHUNK), CHUNK)]

    def scatter(x):
        def to_near(i, _):
            to = i * STRIDE % PLANE
            remote(chunk(x, to), chunk(x, to), sc_s.at[x, 0], sc_r.at[x], to * 2, c).start()
            return 0

        def to_far(i, _):
            to = i * STRIDE % PLANE
            remote(chunk(x, to), chunk(x, to), sc_s.at[x, 1], sc_r.at[x], to * 2 + 1, c).start()
            return 0

        lax.fori_loop(1, PLANE, to_near, 0)
        lax.fori_loop(0, PLANE, to_far, 0)

    def exchange(x):
        def to_one(j, _):
            peer = ((m + j * STRIDE) % PLANE) * 2 + zh

            @pl.when(peer > 0)
            def _():
                remote(chunk(x, m), chunk(x, m), ex_s.at[x], ex_r.at[x], peer, c).start()
            return 0

        lax.fori_loop(1, PLANE, to_one, 0)

    def first_rows(x, n):
        return xb.at[x, pl.ds(0, n * CHUNK)]

    @pl.when(root)
    def _():
        def own_fb(target):
            return remote(fb.at[mine], fb.at[mine], fb_s.at[target], fb_r.at[zl], 0, target * 2 + core)

        own_fb_across = remote(fb.at[mine], fb.at[mine], fb_s.at[4], fb_r.at[4], 0, sib)

        def along_line(up):
            for p, source, target, row in FLOWS:
                if row == 0 and (target > source) == up:
                    @pl.when(zl == source)
                    def _():
                        duty(p, source, target).start()
            for target in (3, 2, 1, 0):
                @pl.when(zl < target if up else zl > target)
                def _():
                    own_fb(target).start()

        get_fb.wait()
        along_line(False)

        @pl.when(zl < 3)
        def _():
            pl.semaphore_wait(above, 3 - zl)
        along_line(True)
        own_fb_across.start()
        get_inv.wait()

        def inverse_on(p, source, core_of):
            piece = invf.at[inverse_rows(p, source, core_of)]
            return remote(piece, piece, on_s.at[p, source], on_r.at[p, source], 0, sib)

        def inverse_arrived(p, source):
            @pl.when(zl != source)
            def _():
                piece = invf.at[inverse_rows(p, source, core)]
                remote(piece, piece, in_s.at[p, 0], in_r.at[p, source], 0, sib).wait_recv()
            inverse_on(p, source, core).start()

        def inverse_times(p, source, right):
            inverse_on(p, source, 1 - core).wait_recv()
            return product(invf[p, source * 128:(source + 1) * 128, 0:(source + 1) * 128], right)

        for i in range(4):
            inverse_arrived(0, i)
        get_b.wait()
        for i in range(4):
            block = inverse_times(0, i, bv[0:(i + 1) * 128])
            o_ref[i * 128:(i + 1) * 128] = block
            xb[0, i * 128:(i + 1) * 128] = block.T
        pl.semaphore_wait(ready, 63)
        scatter(0)
        fb_on = []
        for d in (1, 2, 3):
            source = (zl + d) % 4
            got = fb.at[rows_of(source * 2 + core)]
            remote(got, got, fb_s.at[0], fb_r.at[source], 0, sib).wait_recv()
            on = remote(got, got, fb_s.at[4 + d], fb_r.at[4 + d], 0, sib)
            on.start()
            fb_on.append(on)
        for i in range(4):
            inverse_arrived(1, i)
        for d in range(4):
            (own_fb_across if d == 0 else fb_on[d - 1]).wait_recv()
            shard = pl.ds(pl.multiple_of((zl + d) % 4 * 128, 128), 128)
            bv[512:1024] = bv[512:1024] - product(fb[shard].T, o_ref[shard])
        for i in range(4):
            block = inverse_times(1, i, bv[512:512 + (i + 1) * 128])
            o_ref[512 + i * 128:512 + (i + 1) * 128] = block
            xb[1, i * 128:(i + 1) * 128] = block.T
        scatter(1)
        exchange(1)
        exchange(0)
        for copy in [own_fb_across] + fb_on:
            copy.wait_send()
        for target in range(4):
            @pl.when(zl != target)
            def _():
                own_fb(target).wait_send()
        for p, source, target, row in FLOWS:
            if row == 0:
                @pl.when(zl == source)
                def _():
                    duty(p, source, target).wait_send()
        for p in range(2):
            for i in range(4):
                inverse_on(p, i, core).wait_send()
        for x in range(2):
            for sem in (sc_s.at[x, 0], ex_s.at[x]):
                remote(first_rows(x, 31), first_rows(x, 31), sem, sc_r.at[x], 1, c).wait_send()
            remote(xb.at[x], xb.at[x], sc_s.at[x, 1], sc_r.at[x], 1, c).wait_send()

    def has_source(way, step):
        return zl >= step + 1 if way == 0 else zl <= 2 - step

    def has_target(way):
        return zl <= 2 if way == 0 else zl >= 1

    def shard_at(way, step, p):
        return fall.at[p, rows_of(away(3 - step if way == 0 else 1 + step))]

    def along(way, step, p):
        piece = fall.at[p, mine] if step == 0 else shard_at(way, step - 1, p)
        return remote(piece, piece, ag_s.at[way, step, p], ag_r.at[way, step, p], r, away(1 if way == 0 else 3))

    def arrived(way, step, p):
        piece = shard_at(way, step, p)
        return remote(piece, piece, ag_s.at[way, step, p], ag_r.at[way, step, p], r, sib)

    def across(way, step, p):
        piece = shard_at(way, step, p)
        return remote(piece, piece, sb_s.at[1 + way * 3 + step, p], sb_r.at[1 + way * 3 + step, p], r, sib)

    def own_across(p):
        return remote(fall.at[p, mine], fall.at[p, mine], sb_s.at[0, p], sb_r.at[0, p], r, sib)

    def take(step, p):
        for way in range(2):
            @pl.when(has_source(way, step))
            def _():
                arrived(way, step, p).wait_recv()
                if step < 2:
                    @pl.when(has_target(way))
                    def _():
                        along(way, step + 1, p).start()
                across(way, step, p).start()

    @pl.when(other)
    def _():
        get_f.wait()
        for p in range(2):
            @pl.when(has_target(1))
            def _():
                along(1, 0, p).start()

        @pl.when(has_target(0))
        def _():
            pl.semaphore_wait(above, 1)
            for p in range(2):
                along(0, 0, p).start()
        for p in range(2):
            own_across(p).start()
        take(0, 0)
        take(0, 1)

        def solved(x):
            remote(chunk(x, m), chunk(x, m), sc_s.at[x, 0], sc_r.at[x], 0, c).wait_recv()
            exchange(x)

        solved(0)
        take(1, 0)
        take(1, 1)
        solved(1)
        get_b.wait()
        for x in range(2):
            take(2, x)
            own_across(x).wait_recv()
            for step in range(3):
                for way in range(2):
                    @pl.when(has_source(way, step))
                    def _():
                        across(way, step, x).wait_recv()
            remote(first_rows(x, 31), first_rows(x, 31), ex_s.at[x], ex_r.at[x], 1, c).wait_recv()
            left = jnp.concatenate([xb[x, i * 128:(i + 1) * 128] for i in range(4)], axis=1)

            def update(i, _):
                cut = pl.ds(pl.multiple_of(i * 256, 256), 256)
                took = product(left, fall[x, :, cut])
                if x == 0:
                    total[:, cut] = took
                else:
                    o_ref[cut] = bv[cut] - (total[:, cut] + took).T
                return 0

            lax.fori_loop(0, 4, update, 0)
        for p in range(2):
            own_across(p).wait_send()
            for way in range(2):
                for step in range(3):
                    @pl.when(has_source(way, step))
                    def _():
                        across(way, step, p).wait_send()
                    sent = has_target(way) if step == 0 else has_target(way) & has_source(way, step - 1)

                    @pl.when(sent)
                    def _():
                        along(way, step, p).wait_send()
        for p, source, target, row in FLOWS:
            if row > 0:
                @pl.when((r == row) & (zl == source))
                def _():
                    duty(p, source, target).wait_send()
        for x in range(2):
            @pl.when(zh == 0)
            def _():
                remote(first_rows(x, 30), first_rows(x, 30), ex_s.at[x], ex_r.at[x], 1, c).wait_send()

            @pl.when(zh == 1)
            def _():
                remote(first_rows(x, 31), first_rows(x, 31), ex_s.at[x], ex_r.at[x], 1, c).wait_send()


def on_device(cross_kernel, factor_panels, block_inverses):
    dma = pltpu.SemaphoreType.DMA
    any_space = pl.BlockSpec(memory_space=pl.ANY)
    return pl.pallas_call(
        kernel,
        out_shape=jax.ShapeDtypeStruct(cross_kernel.shape, jnp.float32),
        in_specs=[any_space] * 3,
        out_specs=pl.BlockSpec(memory_space=pltpu.VMEM),
        scratch_shapes=[
            pltpu.VMEM((1024, 128), jnp.float32),
            pltpu.VMEM((2, 512, 1024), jnp.float32),
            pltpu.VMEM((2, 512, 512), jnp.float32),
            pltpu.VMEM((512, 512), jnp.float32),
            pltpu.VMEM((2, 512, 128), jnp.float32),
            pltpu.VMEM((128, 1024), jnp.float32),
            dma((3,)),
            dma((2, 3, 2)), dma((2, 3, 2)),
            dma((7, 2)), dma((7, 2)),
            dma((2, 4)), dma((2, 4)),
            dma((2, 4)), dma((2, 4)),
            dma((8,)), dma((8,)),
            dma((2, 2)), dma((2,)),
            dma((2,)), dma((2,)),
            pltpu.SemaphoreType.REGULAR,
            pltpu.SemaphoreType.REGULAR,
        ],
        compiler_params=pltpu.CompilerParams(
            collective_id=0, has_side_effects=True, vmem_limit_bytes=48 << 20),
    )(*[pltpu.with_memory_space_constraint(x, pltpu.HBM) for x in (cross_kernel, factor_panels, block_inverses)])


def solution(mesh):
    in_specs = (P("rows", "cols"), P(None, "cols", "rows"), P(None, "cols", None))
    out_specs = P("rows", "cols")
    return jax.shard_map(
        on_device, mesh=mesh, in_specs=in_specs, out_specs=out_specs, check_vma=False
    )
```

```python
import jax
import jax.numpy as jnp
from jax import lax
from jax.experimental import pallas as pl
from jax.experimental.pallas import tpu as pltpu
from jax.sharding import PartitionSpec as P

MESH = pl.DeviceIdType.MESH
PLANE = 32
CHUNK = 16
STRIDE = 13
FLOWS = tuple(
    (p, source, target, lines[p])
    for source, target, lines in (
        (1, 0, (0, 4)), (2, 0, (6, 3)), (3, 0, (3, 7)),
        (0, 1, (4, 2)), (2, 1, (2, 6)), (3, 1, (5, 7)),
        (0, 2, (7, 5)), (1, 2, (6, 4)), (3, 2, (2, 4)),
        (0, 3, (3, 5)), (1, 3, (6, 7)), (2, 3, (0, 2)),
    )
    for p in range(2)
)


def halves(value):
    high = value.astype(jnp.bfloat16)
    return high, (value - high.astype(jnp.float32)).astype(jnp.bfloat16)


def product(left, right):
    (a, b), (c, d) = halves(left), halves(right)
    dot = lambda x, y: jnp.dot(x, y, preferred_element_type=jnp.float32)
    return dot(a, c) + (dot(a, d) + dot(b, c))


def kernel(b_hbm, f_hbm, inv_hbm, o_ref, bv, fall, invf, fb, xb, total, loc, ag_s, ag_r, sb_s, sb_r, in_s, in_r, on_s, on_r, fb_s, fb_r, sc_s, sc_r, ex_s, ex_r, ready, above):
    r, c = lax.axis_index("rows"), lax.axis_index("cols")
    m, zh = r // 2, r % 2
    zl, core = c // 2, c % 2
    sib = zl * 2 + 1 - core
    root = r == 0
    other = jnp.logical_not(root)

    def remote(src, dst, s, rs, row, col):
        return pltpu.make_async_remote_copy(
            src_ref=src, dst_ref=dst, send_sem=s, recv_sem=rs,
            device_id={"rows": row, "cols": col}, device_id_type=MESH)

    def away(d):
        return ((zl + d) % 4) * 2 + core

    def rows_of(col):
        return pl.ds(pl.multiple_of(col * 64, 64), 64)

    mine = rows_of(c)
    get_b = pltpu.make_async_copy(b_hbm, bv, loc.at[0])
    get_f = pltpu.make_async_copy(f_hbm, fall.at[:, mine], loc.at[1])
    get_fb = pltpu.make_async_copy(f_hbm.at[0, :, pl.ds(512, 512)], fb.at[mine], loc.at[1])
    get_inv = pltpu.make_async_copy(inv_hbm, invf.at[:, mine], loc.at[2])
    barrier = pltpu.get_barrier_semaphore()

    def tell(row, col):
        pl.semaphore_signal(barrier, inc=1, device_id={"rows": row, "cols": col}, device_id_type=MESH)

    tell(r, sib)

    def open_down(reach):
        for d in range(1, reach + 1):
            @pl.when(zl >= d)
            def _():
                pl.semaphore_signal(above, inc=1, device_id={"rows": r, "cols": c - 2 * d}, device_id_type=MESH)

    @pl.when(root)
    def _():
        for d in range(1, 4):
            @pl.when(zl + d <= 3)
            def _():
                tell(r, c + 2 * d)
        get_fb.start()
        get_inv.start()
        for p, source, target, row in FLOWS:
            if row > 0:
                @pl.when(zl == target)
                def _():
                    tell(row, source * 2 + core)

        def tell_all(j, _):
            tell(2 * PLANE - j, c)
            return 0

        lax.fori_loop(1, 2 * PLANE, tell_all, 0)
        get_b.start()
        pl.semaphore_wait(barrier, zl + 1)
        open_down(3)

    @pl.when(other)
    def _():
        @pl.when(zl < 3)
        def _():
            tell(r, c + 2)
        get_f.start()
        get_b.start()
        duties = sum(((r == row) & (zl == source)).astype(jnp.int32) for p, source, target, row in FLOWS if row > 0)
        pl.semaphore_wait(barrier, jnp.minimum(zl, 1) + 1 + 1 + duties)
        open_down(1)
        pl.semaphore_signal(ready, inc=1, device_id={"rows": 0, "cols": c}, device_id_type=MESH)

    def inverse_rows(p, source, core_of):
        return (p, pl.ds(pl.multiple_of(source * 128 + core_of * 64, 64), 64), pl.ds(0, (source + 1) * 128))

    def duty(p, source, target):
        return remote(
            inv_hbm.at[p, :, pl.ds(0, (source + 1) * 128)], invf.at[inverse_rows(p, source, core)],
            in_s.at[p, target], in_r.at[p, source], 0, target * 2 + core)

    for p, source, target, row in FLOWS:
        if row > 0:
            @pl.when((r == row) & (zl == source))
            def _():
                duty(p, source, target).start()

    def chunk(x, i):
        return xb.at[x, pl.ds(pl.multiple_of(i * CHUNK, CHUNK), CHUNK)]

    def scatter(x):
        def to_near(i, _):
            to = i * STRIDE % PLANE
            remote(chunk(x, to), chunk(x, to), sc_s.at[x, 0], sc_r.at[x], to * 2, c).start()
            return 0

        def to_far(i, _):
            to = i * STRIDE % PLANE
            remote(chunk(x, to), chunk(x, to), sc_s.at[x, 1], sc_r.at[x], to * 2 + 1, c).start()
            return 0

        lax.fori_loop(1, PLANE, to_near, 0)
        lax.fori_loop(0, PLANE, to_far, 0)

    def exchange(x):
        def to_one(j, _):
            peer = ((m + j * STRIDE) % PLANE) * 2 + zh

            @pl.when(peer > 0)
            def _():
                remote(chunk(x, m), chunk(x, m), ex_s.at[x], ex_r.at[x], peer, c).start()
            return 0

        lax.fori_loop(1, PLANE, to_one, 0)

    def first_rows(x, n):
        return xb.at[x, pl.ds(0, n * CHUNK)]

    @pl.when(root)
    def _():
        def own_fb(target):
            return remote(fb.at[mine], fb.at[mine], fb_s.at[target], fb_r.at[zl], 0, target * 2 + core)

        own_fb_across = remote(fb.at[mine], fb.at[mine], fb_s.at[4], fb_r.at[4], 0, sib)

        def along_line(up):
            for p, source, target, row in FLOWS:
                if row == 0 and (target > source) == up:
                    @pl.when(zl == source)
                    def _():
                        duty(p, source, target).start()
            for target in (3, 2, 1, 0):
                @pl.when(zl < target if up else zl > target)
                def _():
                    own_fb(target).start()

        get_fb.wait()
        along_line(False)

        @pl.when(zl < 3)
        def _():
            pl.semaphore_wait(above, 3 - zl)
        along_line(True)
        own_fb_across.start()
        get_inv.wait()

        def inverse_on(p, source, core_of):
            piece = invf.at[inverse_rows(p, source, core_of)]
            return remote(piece, piece, on_s.at[p, source], on_r.at[p, source], 0, sib)

        def inverse_arrived(p, source):
            @pl.when(zl != source)
            def _():
                piece = invf.at[inverse_rows(p, source, core)]
                remote(piece, piece, in_s.at[p, 0], in_r.at[p, source], 0, sib).wait_recv()
            inverse_on(p, source, core).start()

        def inverse_times(p, source, right):
            inverse_on(p, source, 1 - core).wait_recv()
            return product(invf[p, source * 128:(source + 1) * 128, 0:(source + 1) * 128], right)

        for i in range(4):
            inverse_arrived(0, i)
        get_b.wait()
        for i in range(4):
            block = inverse_times(0, i, bv[0:(i + 1) * 128])
            o_ref[i * 128:(i + 1) * 128] = block
            xb[0, i * 128:(i + 1) * 128] = block.T
        pl.semaphore_wait(ready, 63)
        scatter(0)
        fb_on = []
        for d in (1, 2, 3):
            source = (zl + d) % 4
            got = fb.at[rows_of(source * 2 + core)]
            remote(got, got, fb_s.at[0], fb_r.at[source], 0, sib).wait_recv()
            on = remote(got, got, fb_s.at[4 + d], fb_r.at[4 + d], 0, sib)
            on.start()
            fb_on.append(on)
        for i in range(4):
            inverse_arrived(1, i)
        for d in range(4):
            (own_fb_across if d == 0 else fb_on[d - 1]).wait_recv()
            shard = pl.ds(pl.multiple_of((zl + d) % 4 * 128, 128), 128)
            bv[512:1024] = bv[512:1024] - product(fb[shard].T, o_ref[shard])
        for i in range(4):
            block = inverse_times(1, i, bv[512:512 + (i + 1) * 128])
            o_ref[512 + i * 128:512 + (i + 1) * 128] = block
            xb[1, i * 128:(i + 1) * 128] = block.T
        scatter(1)
        exchange(1)
        exchange(0)
        for copy in [own_fb_across] + fb_on:
            copy.wait_send()
        for target in range(4):
            @pl.when(zl != target)
            def _():
                own_fb(target).wait_send()
        for p, source, target, row in FLOWS:
            if row == 0:
                @pl.when(zl == source)
                def _():
                    duty(p, source, target).wait_send()
        for p in range(2):
            for i in range(4):
                inverse_on(p, i, core).wait_send()
        for x in range(2):
            for sem in (sc_s.at[x, 0], ex_s.at[x]):
                remote(first_rows(x, 31), first_rows(x, 31), sem, sc_r.at[x], 1, c).wait_send()
            remote(xb.at[x], xb.at[x], sc_s.at[x, 1], sc_r.at[x], 1, c).wait_send()

    def has_source(way, step):
        return zl >= step + 1 if way == 0 else zl <= 2 - step

    def has_target(way):
        return zl <= 2 if way == 0 else zl >= 1

    def shard_at(way, step, p):
        return fall.at[p, rows_of(away(3 - step if way == 0 else 1 + step))]

    def along(way, step, p):
        piece = fall.at[p, mine] if step == 0 else shard_at(way, step - 1, p)
        return remote(piece, piece, ag_s.at[way, step, p], ag_r.at[way, step, p], r, away(1 if way == 0 else 3))

    def arrived(way, step, p):
        piece = shard_at(way, step, p)
        return remote(piece, piece, ag_s.at[way, step, p], ag_r.at[way, step, p], r, sib)

    def across(way, step, p):
        piece = shard_at(way, step, p)
        return remote(piece, piece, sb_s.at[1 + way * 3 + step, p], sb_r.at[1 + way * 3 + step, p], r, sib)

    def own_across(p):
        return remote(fall.at[p, mine], fall.at[p, mine], sb_s.at[0, p], sb_r.at[0, p], r, sib)

    def take(step, p):
        for way in range(2):
            @pl.when(has_source(way, step))
            def _():
                arrived(way, step, p).wait_recv()
                if step < 2:
                    @pl.when(has_target(way))
                    def _():
                        along(way, step + 1, p).start()
                across(way, step, p).start()

    @pl.when(other)
    def _():
        get_f.wait()
        for p in range(2):
            @pl.when(has_target(1))
            def _():
                along(1, 0, p).start()

        @pl.when(has_target(0))
        def _():
            pl.semaphore_wait(above, 1)
            for p in range(2):
                along(0, 0, p).start()
        for p in range(2):
            own_across(p).start()
        take(0, 0)
        take(0, 1)

        def solved(x):
            remote(chunk(x, m), chunk(x, m), sc_s.at[x, 0], sc_r.at[x], 0, c).wait_recv()
            exchange(x)

        solved(0)
        take(1, 0)
        take(1, 1)
        solved(1)
        get_b.wait()
        for x in range(2):
            take(2, x)
            own_across(x).wait_recv()
            for step in range(3):
                for way in range(2):
                    @pl.when(has_source(way, step))
                    def _():
                        across(way, step, x).wait_recv()
            remote(first_rows(x, 31), first_rows(x, 31), ex_s.at[x], ex_r.at[x], 1, c).wait_recv()
            left = jnp.concatenate([xb[x, i * 128:(i + 1) * 128] for i in range(4)], axis=1)

            def update(i, _):
                cut = pl.ds(pl.multiple_of(i * 256, 256), 256)
                took = product(left, fall[x, :, cut])
                if x == 0:
                    total[:, cut] = took
                else:
                    o_ref[cut] = bv[cut] - (total[:, cut] + took).T
                return 0

            lax.fori_loop(0, 4, update, 0)
        for p in range(2):
            own_across(p).wait_send()
            for way in range(2):
                for step in range(3):
                    @pl.when(has_source(way, step))
                    def _():
                        across(way, step, p).wait_send()
                    sent = has_target(way) if step == 0 else has_target(way) & has_source(way, step - 1)

                    @pl.when(sent)
                    def _():
                        along(way, step, p).wait_send()
        for p, source, target, row in FLOWS:
            if row > 0:
                @pl.when((r == row) & (zl == source))
                def _():
                    duty(p, source, target).wait_send()
        for x in range(2):
            @pl.when(zh == 0)
            def _():
                remote(first_rows(x, 30), first_rows(x, 30), ex_s.at[x], ex_r.at[x], 1, c).wait_send()

            @pl.when(zh == 1)
            def _():
                remote(first_rows(x, 31), first_rows(x, 31), ex_s.at[x], ex_r.at[x], 1, c).wait_send()


def on_device(cross_kernel, factor_panels, block_inverses):
    dma = pltpu.SemaphoreType.DMA
    any_space = pl.BlockSpec(memory_space=pl.ANY)
    return pl.pallas_call(
        kernel,
        out_shape=jax.ShapeDtypeStruct(cross_kernel.shape, jnp.float32),
        in_specs=[any_space] * 3,
        out_specs=pl.BlockSpec(memory_space=pltpu.VMEM),
        scratch_shapes=[
            pltpu.VMEM((1024, 128), jnp.float32),
            pltpu.VMEM((2, 512, 1024), jnp.float32),
            pltpu.VMEM((2, 512, 512), jnp.float32),
            pltpu.VMEM((512, 512), jnp.float32),
            pltpu.VMEM((2, 512, 128), jnp.float32),
            pltpu.VMEM((128, 1024), jnp.float32),
            dma((3,)),
            dma((2, 3, 2)), dma((2, 3, 2)),
            dma((7, 2)), dma((7, 2)),
            dma((2, 4)), dma((2, 4)),
            dma((2, 4)), dma((2, 4)),
            dma((8,)), dma((8,)),
            dma((2, 2)), dma((2,)),
            dma((2,)), dma((2,)),
            pltpu.SemaphoreType.REGULAR,
            pltpu.SemaphoreType.REGULAR,
        ],
        compiler_params=pltpu.CompilerParams(
            collective_id=0, has_side_effects=True, vmem_limit_bytes=48 << 20),
    )(*[pltpu.with_memory_space_constraint(x, pltpu.HBM) for x in (cross_kernel, factor_panels, block_inverses)])


def solution(mesh):
    in_specs = (P("rows", "cols"), P(None, "cols", "rows"), P(None, "cols", None))
    out_specs = P("rows", "cols")
    return jax.shard_map(
        on_device, mesh=mesh, in_specs=in_specs, out_specs=out_specs, check_vma=False
    )
```

```python
import jax
import jax.numpy as jnp
from jax import lax
from jax.experimental import pallas as pl
from jax.experimental.pallas import tpu as pltpu
from jax.sharding import PartitionSpec as P

MESH = pl.DeviceIdType.MESH
PLANE = 32
CHUNK = 16
STRIDE = 21
FLOWS = tuple(
    (p, source, target, lines[p])
    for source, target, lines in (
        (1, 0, (2, 4)), (2, 0, (6, 3)), (3, 0, (3, 7)),
        (0, 1, (4, 2)), (2, 1, (2, 6)), (3, 1, (5, 7)),
        (0, 2, (7, 5)), (1, 2, (6, 4)), (3, 2, (2, 4)),
        (0, 3, (3, 5)), (1, 3, (6, 7)), (2, 3, (4, 2)),
    )
    for p in range(2)
)


def halves(value):
    high = value.astype(jnp.bfloat16)
    return high, (value - high.astype(jnp.float32)).astype(jnp.bfloat16)


def product(left, right):
    (a, b), (c, d) = halves(left), halves(right)
    dot = lambda x, y: jnp.dot(x, y, preferred_element_type=jnp.float32)
    return dot(a, c) + (dot(a, d) + dot(b, c))


def kernel(b_hbm, f_hbm, inv_hbm, o_ref, bv, fall, invf, fb, xb, total, loc, ag_s, ag_r, sb_s, sb_r, in_s, in_r, on_s, on_r, fb_s, fb_r, sc_s, sc_r, ex_s, ex_r, ready, above):
    r, c = lax.axis_index("rows"), lax.axis_index("cols")
    m, zh = r // 2, r % 2
    zl, core = c // 2, c % 2
    sib = zl * 2 + 1 - core
    root = r == 0
    other = jnp.logical_not(root)

    def remote(src, dst, s, rs, row, col):
        return pltpu.make_async_remote_copy(
            src_ref=src, dst_ref=dst, send_sem=s, recv_sem=rs,
            device_id={"rows": row, "cols": col}, device_id_type=MESH)

    def away(d):
        return ((zl + d) % 4) * 2 + core

    def rows_of(col):
        return pl.ds(pl.multiple_of(col * 64, 64), 64)

    mine = rows_of(c)
    get_b = pltpu.make_async_copy(b_hbm, bv, loc.at[0])
    get_f = pltpu.make_async_copy(f_hbm, fall.at[:, mine], loc.at[1])
    get_fb = pltpu.make_async_copy(f_hbm.at[0, :, pl.ds(512, 512)], fb.at[mine], loc.at[1])
    get_inv = pltpu.make_async_copy(inv_hbm, invf.at[:, mine], loc.at[2])
    barrier = pltpu.get_barrier_semaphore()

    def tell(row, col):
        pl.semaphore_signal(barrier, inc=1, device_id={"rows": row, "cols": col}, device_id_type=MESH)

    tell(r, sib)

    def open_down(reach):
        for d in range(1, reach + 1):
            @pl.when(zl >= d)
            def _():
                pl.semaphore_signal(above, inc=1, device_id={"rows": r, "cols": c - 2 * d}, device_id_type=MESH)

    @pl.when(root)
    def _():
        for d in range(1, 4):
            @pl.when(zl + d <= 3)
            def _():
                tell(r, c + 2 * d)
        get_fb.start()
        get_inv.start()
        for p, source, target, row in FLOWS:
            if row > 0:
                @pl.when(zl == target)
                def _():
                    tell(row, source * 2 + core)

        def tell_all(j, _):
            tell(2 * PLANE - j, c)
            return 0

        lax.fori_loop(1, 2 * PLANE, tell_all, 0)
        get_b.start()
        pl.semaphore_wait(barrier, zl + 1)
        open_down(3)

    @pl.when(other)
    def _():
        @pl.when(zl < 3)
        def _():
            tell(r, c + 2)
        get_f.start()
        get_b.start()
        duties = sum(((r == row) & (zl == source)).astype(jnp.int32) for p, source, target, row in FLOWS if row > 0)
        pl.semaphore_wait(barrier, jnp.minimum(zl, 1) + 1 + 1 + duties)
        open_down(1)
        pl.semaphore_signal(ready, inc=1, device_id={"rows": 0, "cols": c}, device_id_type=MESH)

    def inverse_rows(p, source, core_of):
        return (p, pl.ds(pl.multiple_of(source * 128 + core_of * 64, 64), 64), pl.ds(0, (source + 1) * 128))

    def duty(p, source, target):
        return remote(
            inv_hbm.at[p, :, pl.ds(0, (source + 1) * 128)], invf.at[inverse_rows(p, source, core)],
            in_s.at[p, target], in_r.at[p, source], 0, target * 2 + core)

    for p, source, target, row in FLOWS:
        if row > 0:
            @pl.when((r == row) & (zl == source))
            def _():
                duty(p, source, target).start()

    def chunk(x, i):
        return xb.at[x, pl.ds(pl.multiple_of(i * CHUNK, CHUNK), CHUNK)]

    def scatter(x):
        def to_near(i, _):
            to = i * STRIDE % PLANE
            remote(chunk(x, to), chunk(x, to), sc_s.at[x, 0], sc_r.at[x], to * 2, c).start()
            return 0

        def to_far(i, _):
            to = i * STRIDE % PLANE
            remote(chunk(x, to), chunk(x, to), sc_s.at[x, 1], sc_r.at[x], to * 2 + 1, c).start()
            return 0

        lax.fori_loop(1, PLANE, to_near, 0)
        lax.fori_loop(0, PLANE, to_far, 0)

    def exchange(x):
        def to_one(j, _):
            peer = ((m + j * STRIDE) % PLANE) * 2 + zh

            @pl.when(peer > 0)
            def _():
                remote(chunk(x, m), chunk(x, m), ex_s.at[x], ex_r.at[x], peer, c).start()
            return 0

        lax.fori_loop(1, PLANE, to_one, 0)

    def first_rows(x, n):
        return xb.at[x, pl.ds(0, n * CHUNK)]

    @pl.when(root)
    def _():
        def own_fb(target):
            return remote(fb.at[mine], fb.at[mine], fb_s.at[target], fb_r.at[zl], 0, target * 2 + core)

        own_fb_across = remote(fb.at[mine], fb.at[mine], fb_s.at[4], fb_r.at[4], 0, sib)

        def along_line(up):
            for p, source, target, row in FLOWS:
                if row == 0 and (target > source) == up:
                    @pl.when(zl == source)
                    def _():
                        duty(p, source, target).start()
            for target in (3, 2, 1, 0):
                @pl.when(zl < target if up else zl > target)
                def _():
                    own_fb(target).start()

        get_fb.wait()
        along_line(False)

        @pl.when(zl < 3)
        def _():
            pl.semaphore_wait(above, 3 - zl)
        along_line(True)
        own_fb_across.start()
        get_inv.wait()

        def inverse_on(p, source, core_of):
            piece = invf.at[inverse_rows(p, source, core_of)]
            return remote(piece, piece, on_s.at[p, source], on_r.at[p, source], 0, sib)

        def inverse_arrived(p, source):
            @pl.when(zl != source)
            def _():
                piece = invf.at[inverse_rows(p, source, core)]
                remote(piece, piece, in_s.at[p, 0], in_r.at[p, source], 0, sib).wait_recv()
            inverse_on(p, source, core).start()

        def inverse_times(p, source, right):
            inverse_on(p, source, 1 - core).wait_recv()
            return product(invf[p, source * 128:(source + 1) * 128, 0:(source + 1) * 128], right)

        for i in range(4):
            inverse_arrived(0, i)
        get_b.wait()
        for i in range(4):
            block = inverse_times(0, i, bv[0:(i + 1) * 128])
            o_ref[i * 128:(i + 1) * 128] = block
            xb[0, i * 128:(i + 1) * 128] = block.T
        pl.semaphore_wait(ready, 63)
        scatter(0)
        fb_on = []
        for d in (1, 2, 3):
            source = (zl + d) % 4
            got = fb.at[rows_of(source * 2 + core)]
            remote(got, got, fb_s.at[0], fb_r.at[source], 0, sib).wait_recv()
            on = remote(got, got, fb_s.at[4 + d], fb_r.at[4 + d], 0, sib)
            on.start()
            fb_on.append(on)
        for i in range(4):
            inverse_arrived(1, i)
        for d in range(4):
            (own_fb_across if d == 0 else fb_on[d - 1]).wait_recv()
            shard = pl.ds(pl.multiple_of((zl + d) % 4 * 128, 128), 128)
            bv[512:1024] = bv[512:1024] - product(fb[shard].T, o_ref[shard])
        for i in range(4):
            block = inverse_times(1, i, bv[512:512 + (i + 1) * 128])
            o_ref[512 + i * 128:512 + (i + 1) * 128] = block
            xb[1, i * 128:(i + 1) * 128] = block.T
        scatter(1)
        exchange(1)
        exchange(0)
        for copy in [own_fb_across] + fb_on:
            copy.wait_send()
        for target in range(4):
            @pl.when(zl != target)
            def _():
                own_fb(target).wait_send()
        for p, source, target, row in FLOWS:
            if row == 0:
                @pl.when(zl == source)
                def _():
                    duty(p, source, target).wait_send()
        for p in range(2):
            for i in range(4):
                inverse_on(p, i, core).wait_send()
        for x in range(2):
            for sem in (sc_s.at[x, 0], ex_s.at[x]):
                remote(first_rows(x, 31), first_rows(x, 31), sem, sc_r.at[x], 1, c).wait_send()
            remote(xb.at[x], xb.at[x], sc_s.at[x, 1], sc_r.at[x], 1, c).wait_send()

    def has_source(way, step):
        return zl >= step + 1 if way == 0 else zl <= 2 - step

    def has_target(way):
        return zl <= 2 if way == 0 else zl >= 1

    def shard_at(way, step, p):
        return fall.at[p, rows_of(away(3 - step if way == 0 else 1 + step))]

    def along(way, step, p):
        piece = fall.at[p, mine] if step == 0 else shard_at(way, step - 1, p)
        return remote(piece, piece, ag_s.at[way, step, p], ag_r.at[way, step, p], r, away(1 if way == 0 else 3))

    def arrived(way, step, p):
        piece = shard_at(way, step, p)
        return remote(piece, piece, ag_s.at[way, step, p], ag_r.at[way, step, p], r, sib)

    def across(way, step, p):
        piece = shard_at(way, step, p)
        return remote(piece, piece, sb_s.at[1 + way * 3 + step, p], sb_r.at[1 + way * 3 + step, p], r, sib)

    def own_across(p):
        return remote(fall.at[p, mine], fall.at[p, mine], sb_s.at[0, p], sb_r.at[0, p], r, sib)

    def take(step, p):
        for way in range(2):
            @pl.when(has_source(way, step))
            def _():
                arrived(way, step, p).wait_recv()
                if step < 2:
                    @pl.when(has_target(way))
                    def _():
                        along(way, step + 1, p).start()
                across(way, step, p).start()

    @pl.when(other)
    def _():
        get_f.wait()
        for p in range(2):
            @pl.when(has_target(1))
            def _():
                along(1, 0, p).start()

        @pl.when(has_target(0))
        def _():
            pl.semaphore_wait(above, 1)
            for p in range(2):
                along(0, 0, p).start()
        for p in range(2):
            own_across(p).start()
        take(0, 0)
        take(0, 1)

        def solved(x):
            remote(chunk(x, m), chunk(x, m), sc_s.at[x, 0], sc_r.at[x], 0, c).wait_recv()
            exchange(x)

        solved(0)
        take(1, 0)
        take(1, 1)
        solved(1)
        get_b.wait()
        for x in range(2):
            take(2, x)
            own_across(x).wait_recv()
            for step in range(3):
                for way in range(2):
                    @pl.when(has_source(way, step))
                    def _():
                        across(way, step, x).wait_recv()
            remote(first_rows(x, 31), first_rows(x, 31), ex_s.at[x], ex_r.at[x], 1, c).wait_recv()
            left = jnp.concatenate([xb[x, i * 128:(i + 1) * 128] for i in range(4)], axis=1)

            def update(i, _):
                cut = pl.ds(pl.multiple_of(i * 256, 256), 256)
                took = product(left, fall[x, :, cut])
                if x == 0:
                    total[:, cut] = took
                else:
                    o_ref[cut] = bv[cut] - (total[:, cut] + took).T
                return 0

            lax.fori_loop(0, 4, update, 0)
        for p in range(2):
            own_across(p).wait_send()
            for way in range(2):
                for step in range(3):
                    @pl.when(has_source(way, step))
                    def _():
                        across(way, step, p).wait_send()
                    sent = has_target(way) if step == 0 else has_target(way) & has_source(way, step - 1)

                    @pl.when(sent)
                    def _():
                        along(way, step, p).wait_send()
        for p, source, target, row in FLOWS:
            if row > 0:
                @pl.when((r == row) & (zl == source))
                def _():
                    duty(p, source, target).wait_send()
        for x in range(2):
            @pl.when(zh == 0)
            def _():
                remote(first_rows(x, 30), first_rows(x, 30), ex_s.at[x], ex_r.at[x], 1, c).wait_send()

            @pl.when(zh == 1)
            def _():
                remote(first_rows(x, 31), first_rows(x, 31), ex_s.at[x], ex_r.at[x], 1, c).wait_send()


def on_device(cross_kernel, factor_panels, block_inverses):
    dma = pltpu.SemaphoreType.DMA
    any_space = pl.BlockSpec(memory_space=pl.ANY)
    return pl.pallas_call(
        kernel,
        out_shape=jax.ShapeDtypeStruct(cross_kernel.shape, jnp.float32),
        in_specs=[any_space] * 3,
        out_specs=pl.BlockSpec(memory_space=pltpu.VMEM),
        scratch_shapes=[
            pltpu.VMEM((1024, 128), jnp.float32),
            pltpu.VMEM((2, 512, 1024), jnp.float32),
            pltpu.VMEM((2, 512, 512), jnp.float32),
            pltpu.VMEM((512, 512), jnp.float32),
            pltpu.VMEM((2, 512, 128), jnp.float32),
            pltpu.VMEM((128, 1024), jnp.float32),
            dma((3,)),
            dma((2, 3, 2)), dma((2, 3, 2)),
            dma((7, 2)), dma((7, 2)),
            dma((2, 4)), dma((2, 4)),
            dma((2, 4)), dma((2, 4)),
            dma((8,)), dma((8,)),
            dma((2, 2)), dma((2,)),
            dma((2,)), dma((2,)),
            pltpu.SemaphoreType.REGULAR,
            pltpu.SemaphoreType.REGULAR,
        ],
        compiler_params=pltpu.CompilerParams(
            collective_id=0, has_side_effects=True, vmem_limit_bytes=48 << 20),
    )(*[pltpu.with_memory_space_constraint(x, pltpu.HBM) for x in (cross_kernel, factor_panels, block_inverses)])


def solution(mesh):
    in_specs = (P("rows", "cols"), P(None, "cols", "rows"), P(None, "cols", None))
    out_specs = P("rows", "cols")
    return jax.shard_map(
        on_device, mesh=mesh, in_specs=in_specs, out_specs=out_specs, check_vma=False
    )
```
